32 devices in a mesh: dp: 16 (over z, y, core), tensor: 2 (over x).
Axes of the slice: x: 2, y: 2, z: 4, core: 2. Of those that a mesh axis runs over, the one named last changes fastest.
Arguments:
- tokens: bfloat16 [4096, 6144], P('dp', 'tensor'), may hold values from -6 to 6
- grad_out: bfloat16 [4096, 6144], P('dp', 'tensor'), may hold values from -6 to 6
- input_norm_gain: float32 [6144], replicated, may hold values from 0.1 to 1.9
- q_gain: float32 [128], replicated, may hold values from 0.1 to 1.9
- k_gain: float32 [128], replicated, may hold values from 0.1 to 1.9
- w_qkv: bfloat16 [3, 6144, 3072], P(None, 'dp', 'tensor'), may hold values from -0.078125 to 0.078125
- w_out: bfloat16 [3072, 6144], P('tensor', 'dp'), may hold values from -0.109375 to 0.109375
- pattern: int32 [24, 4, 2], P('tensor'), may hold values from 0 to 3, all different within a row
Outputs:
- tokens_grad: bfloat16 [4096, 6144], P('dp', 'tensor')
The draws below stay inside these ranges and needn't reach their ends.
All inputs are finite; a program needn't handle non-finite values.
Results may differ from the reference program's by a relative error of at most 0.015.
Values may be sent and summed in bfloat16 or wider, within the bound.
A program may use at most 192 MiB of HBM per device.

```python
import math
import jax
import jax.numpy as jnp
from jax import lax

D = 6144
HEADS = 24
HD = 128
SEQ = 256
BLK = 64
KSEL = 2
NQB = 4
TOKENS = 4096


def level_of(own_key, extent, cuts, least, high):
    factor_of = 1.0
    for position, parts in cuts:
        heights = jax.random.uniform(jax.random.fold_in(jax.random.fold_in(own_key, 6), position), (parts,), jnp.float32, least / len(cuts), high / len(cuts))
        factor_of = factor_of * jnp.repeat(jnp.exp(heights), extent[position] // parts).reshape((-1,) + (1,) * (len(extent) - 1 - position))
    return factor_of


def distinct(own_key, rows, number_of, top, lift):
    ranking = jax.random.permutation(jax.random.fold_in(own_key, 1), number_of)
    boost = ranking
    for power in range(3):
        boost = boost * boost // number_of
    boost = boost * lift // number_of
    tickets = jax.random.randint(jax.random.fold_in(own_key, 2), (rows, number_of), 0, 4096) + boost
    fixed_rows = jax.random.permutation(jax.random.fold_in(own_key, 3), rows)[jnp.arange(number_of) % rows]
    tickets = jnp.where(jnp.arange(rows)[:, None] == fixed_rows[None, :], 1 << 14, tickets)
    score = tickets * number_of + jnp.arange(number_of)
    return lax.top_k(score.astype(jnp.int32), top)[1].astype(jnp.int32)


def bell_draw(key, extent, deviation, most, pieces=(), kind=jnp.bfloat16):
    array = deviation * jax.random.normal(key, extent, jnp.float32)
    if pieces:
        array = array * level_of(key, extent, pieces, -0.22, 0.18)
    return jnp.clip(array, -most, most).astype(kind)


def setup_inputs(seed: int = 0) -> dict:
    key_of = jax.random.split(jax.random.key(seed), 9)
    tokens = bell_draw(key_of[0], (TOKENS, D), 1.0, 6.0, ((0, 16), (1, 2)))
    grad_out = bell_draw(key_of[1], (TOKENS, D), 1.0, 6.0, ((0, 16), (1, 2)))
    input_norm_gain = jnp.clip(1.0 + 0.18 * jax.random.normal(key_of[2], (D,), jnp.float32), 0.1, 1.9)
    q_gain = jnp.clip(1.0 + 0.18 * jax.random.normal(key_of[3], (HD,), jnp.float32), 0.1, 1.9)
    k_gain = jnp.clip(1.0 + 0.18 * jax.random.normal(key_of[4], (HD,), jnp.float32), 0.1, 1.9)
    w_qkv = bell_draw(key_of[5], (3, D, HEADS * HD), D ** -0.5, 0.078125, ((1, 16), (2, 2)))
    w_out = bell_draw(key_of[6], (HEADS * HD, D), (HEADS * HD) ** -0.5, 0.109375, ((0, 2), (1, 16)))
    pattern = distinct(key_of[7], HEADS * NQB, NQB, KSEL, 0).reshape((HEADS, NQB, KSEL))
    return {"tokens": tokens, "grad_out": grad_out, "input_norm_gain": input_norm_gain, "q_gain": q_gain, "k_gain": k_gain, "w_qkv": w_qkv, "w_out": w_out, "pattern": pattern}


def norm_rows(values, gain):
    centre = lax.optimization_barrier(jnp.mean(values, axis=-1, keepdims=True))
    centered_input = values - centre
    inverse_deviation = lax.rsqrt(lax.optimization_barrier(jnp.mean(centered_input * centered_input, axis=-1, keepdims=True)) + 1e-06)
    return centered_input * inverse_deviation * gain

def block_mask(pattern, seq_len, block):
    count = seq_len // block
    hits = pattern[:, :, :, None] == jnp.arange(count, dtype=jnp.int32)[None, None, None, :]
    allowed = jnp.any(hits, axis=2).astype(jnp.float32)
    heads = allowed.shape[0]
    spread = jnp.broadcast_to(allowed[:, :, None, :, None], (heads, count, block, count, block))
    return spread.reshape(heads, seq_len, seq_len)

def attention_grads(stacked, upstream, q_gain, k_gain, allowed):

    def attend(query, key, value):
        q_normed = norm_rows(query, q_gain)
        k_normed = norm_rows(key, k_gain)
        scores = jnp.einsum('aqhd,akhd->ahqk', q_normed, k_normed, precision=lax.Precision.HIGHEST) / math.sqrt(query.shape[-1])
        weights = jnp.exp(scores) * allowed[None]
        probs = weights / lax.optimization_barrier(jnp.sum(weights, axis=-1, keepdims=True))
        return jnp.einsum('ahqk,akhd->aqhd', probs, value, precision=lax.Precision.HIGHEST)
    widened = stacked.astype(jnp.float32)
    _, pull = jax.vjp(attend, widened[0], widened[1], widened[2])
    grads = pull(upstream.astype(jnp.float32))
    return jnp.stack(grads).astype(jnp.bfloat16)

def reference(tokens, grad_out, input_norm_gain, q_gain, k_gain, w_qkv, w_out, pattern):
    allowed = block_mask(pattern, SEQ, BLK)

    def one_image(pair):
        rows, grads = pair
        values = rows.astype(jnp.float32)
        centre = lax.optimization_barrier(jnp.mean(values, axis=-1, keepdims=True))
        centered_input = values - centre
        inverse_deviation = lax.rsqrt(lax.optimization_barrier(jnp.mean(centered_input * centered_input, axis=-1, keepdims=True)) + 1e-06)
        standardized_input = centered_input * inverse_deviation
        normalized_input = (standardized_input * input_norm_gain).astype(jnp.bfloat16)
        qkv = jnp.stack([jnp.dot(normalized_input, w_qkv[index], preferred_element_type=jnp.float32) for index in range(3)]).astype(jnp.bfloat16)
        upstream = lax.dot_general(grads, w_out, (((1,), (1,)), ((), ())), preferred_element_type=jnp.float32).astype(jnp.bfloat16)
        heads_view = qkv.reshape(3, 1, SEQ, HEADS, HD)
        d_qkv = attention_grads(heads_view, upstream.reshape(1, SEQ, HEADS, HD), q_gain, k_gain, allowed).reshape(3, SEQ, HEADS * HD)
        d_normed = jnp.zeros((SEQ, D), jnp.float32)
        for index in range(3):
            d_normed = d_normed + lax.dot_general(d_qkv[index], w_qkv[index], (((1,), (1,)), ((), ())), preferred_element_type=jnp.float32)
        normalized_gradient = d_normed * input_norm_gain
        leading_term = lax.optimization_barrier(jnp.mean(normalized_gradient, axis=-1, keepdims=True))
        trailing_term = lax.optimization_barrier(jnp.mean(normalized_gradient * standardized_input, axis=-1, keepdims=True))
        return (inverse_deviation * (normalized_gradient - leading_term - standardized_input * trailing_term)).astype(jnp.bfloat16)
    images = tokens.reshape(-1, SEQ, D)
    grad_images = grad_out.reshape(-1, SEQ, D)
    result = lax.map(one_image, (images, grad_images))
    return result.reshape(tokens.shape)
```

```python
import functools
import math

import jax
import jax.numpy as jnp
from jax import lax
from jax.experimental import pallas as pl
from jax.experimental.pallas import tpu as pltpu
from jax.sharding import PartitionSpec as P

HD = 128
SEQ = 256
BLK = 64
EPS = 1e-06


def attention_kernel(heads, ksel, pattern_ref, q_gain_ref, k_gain_ref, qkv_ref, up_ref, out_ref):
    width = heads * HD
    scale = 1.0 / math.sqrt(HD)
    q_gain = q_gain_ref[...]
    k_gain = k_gain_ref[...]
    blocks = SEQ // BLK
    column_block = lax.broadcasted_iota(jnp.int32, (BLK, SEQ), 1) // BLK

    def normalize(values):
        centred = values - jnp.mean(values, axis=-1, keepdims=True)
        inverse = lax.rsqrt(jnp.mean(centred * centred, axis=-1, keepdims=True) + EPS)
        return centred * inverse, inverse

    def pull_back(grad, hat, inverse, gain):
        d_hat = grad * gain
        return inverse * (
            d_hat
            - jnp.mean(d_hat, axis=-1, keepdims=True)
            - hat * jnp.mean(d_hat * hat, axis=-1, keepdims=True)
        )

    def dot(a, b, dims, precision=None):
        return lax.dot_general(
            a, b, (dims, ((), ())), precision=precision, preferred_element_type=jnp.float32
        )

    for head in range(heads):
        lo = head * HD
        q_hat, q_inverse = normalize(qkv_ref[:, lo : lo + HD].astype(jnp.float32))
        k_hat, k_inverse = normalize(
            qkv_ref[:, width + lo : width + lo + HD].astype(jnp.float32)
        )
        value = qkv_ref[:, 2 * width + lo : 2 * width + lo + HD]
        upstream = up_ref[:, lo : lo + HD]
        q_normed = q_hat * q_gain
        k_normed = k_hat * k_gain
        scores = dot(q_normed * scale, k_normed, ((1,), (1,)), lax.Precision.HIGHEST)
        rows = []
        for i in range(blocks):
            hit = column_block == pattern_ref[(head * blocks + i) * ksel]
            for s in range(1, ksel):
                hit = hit | (column_block == pattern_ref[(head * blocks + i) * ksel + s])
            rows.append(jnp.where(hit, jnp.exp(scores[i * BLK : (i + 1) * BLK]), 0.0))
        weights = jnp.concatenate(rows, axis=0)
        probs = weights / jnp.sum(weights, axis=-1, keepdims=True)
        d_probs = dot(upstream, value, ((1,), (1,)))
        d_value = dot(probs.astype(jnp.bfloat16), upstream, ((0,), (0,)))
        d_scores = probs * (d_probs - jnp.sum(probs * d_probs, axis=-1, keepdims=True))
        d_scores = (d_scores * scale).astype(jnp.bfloat16)
        d_q = dot(d_scores, k_normed.astype(jnp.bfloat16), ((1,), (0,)))
        d_k = dot(d_scores, q_normed.astype(jnp.bfloat16), ((0,), (0,)))
        out_ref[:, lo : lo + HD] = pull_back(d_q, q_hat, q_inverse, q_gain).astype(jnp.bfloat16)
        out_ref[:, width + lo : width + lo + HD] = pull_back(
            d_k, k_hat, k_inverse, k_gain
        ).astype(jnp.bfloat16)
        out_ref[:, 2 * width + lo : 2 * width + lo + HD] = d_value.astype(jnp.bfloat16)


def attention_grads(qkv, upstream, q_gain, k_gain, pattern):
    rows, width = upstream.shape
    heads = width // HD
    images = rows // SEQ
    return pl.pallas_call(
        functools.partial(attention_kernel, heads, pattern.shape[2]),
        grid=(images,),
        out_shape=jax.ShapeDtypeStruct((rows, 3 * width), jnp.bfloat16),
        in_specs=[
            pl.BlockSpec(memory_space=pltpu.SMEM),
            pl.BlockSpec((1, HD), lambda i: (0, 0)),
            pl.BlockSpec((1, HD), lambda i: (0, 0)),
            pl.BlockSpec((SEQ, 3 * width), lambda i: (i, 0)),
            pl.BlockSpec((SEQ, width), lambda i: (i, 0)),
        ],
        out_specs=pl.BlockSpec((SEQ, 3 * width), lambda i: (i, 0)),
        cost_estimate=pl.CostEstimate(
            flops=images * heads * 20 * SEQ * SEQ * HD,
            bytes_accessed=rows * width * 14,
            transcendentals=images * heads * SEQ * SEQ,
        ),
    )(pattern.reshape(-1), q_gain.reshape(1, HD), k_gain.reshape(1, HD), qkv, upstream)


def head_chunks(heads):
    sizes = []
    left = heads - 1
    while left > 0:
        take = min(4, left)
        sizes.append(take)
        left -= take
    return sizes + [1]


def body(tokens, grad_out, input_norm_gain, q_gain, k_gain, w_qkv, w_out, pattern):
    row_count, width = tokens.shape
    parts = lax.axis_size("tensor")
    me = lax.axis_index("tensor")
    local_heads = w_qkv.shape[2] // HD

    w_out_t = w_out.T
    gathered = []
    start = 0
    sizes = head_chunks(local_heads)
    for size in sizes:
        cols = slice(start * HD, (start + size) * HD)
        piece = jnp.concatenate(
            [w_qkv[0, :, cols], w_qkv[1, :, cols], w_qkv[2, :, cols], w_out_t[:, cols]], axis=1
        )
        gathered.append(lax.all_gather(piece, "dp", axis=0, tiled=True))
        start += size

    def exchange(value, shift):
        return lax.ppermute(
            value, "tensor", [(source, (source + shift) % parts) for source in range(parts)]
        )

    def whole_rows(own):
        full = jnp.zeros((row_count, width * parts), own.dtype)
        full = lax.dynamic_update_slice_in_dim(full, own, me * width, 1)
        for shift in range(1, parts):
            full = lax.dynamic_update_slice_in_dim(
                full, exchange(own, shift), lax.rem(me + parts - shift, parts) * width, 1
            )
        return full

    values = whole_rows(tokens).astype(jnp.float32)
    grads_full = whole_rows(grad_out)
    centre = jnp.mean(values, axis=-1, keepdims=True)
    centred = values - centre
    inverse = lax.rsqrt(jnp.mean(centred * centred, axis=-1, keepdims=True) + EPS)
    hat = centred * inverse
    normed = (hat * input_norm_gain).astype(jnp.bfloat16)

    def own_columns(array, index, axis):
        return lax.dynamic_slice_in_dim(array, index * width, width, axis)

    targets = [lax.rem(me + shift, parts) for shift in range(parts)]
    totals = [None] * parts
    start = 0
    for size, weight in zip(sizes, gathered):
        span = size * HD
        qkv = jnp.dot(
            normed, weight[:, : 3 * span], preferred_element_type=jnp.float32
        ).astype(jnp.bfloat16)
        upstream = jnp.dot(
            grads_full, weight[:, 3 * span :], preferred_element_type=jnp.float32
        ).astype(jnp.bfloat16)
        d_qkv = attention_grads(
            qkv, upstream, q_gain, k_gain, pattern[start : start + size]
        )
        for shift in range(parts):
            term = lax.dot_general(
                d_qkv,
                own_columns(weight, targets[shift], 0)[:, : 3 * span],
                (((1,), (1,)), ((), ())),
                preferred_element_type=jnp.float32,
            )
            totals[shift] = term if totals[shift] is None else totals[shift] + term
        start += size

    received = [exchange(totals[shift].astype(jnp.bfloat16), shift) for shift in range(1, parts)]
    sums = jnp.zeros((row_count, 2), jnp.float32)
    for shift in range(parts):
        gain = own_columns(input_norm_gain, targets[shift], 0)
        scaled = totals[shift] * gain
        sums = sums + jnp.stack(
            [
                jnp.sum(scaled, axis=-1),
                jnp.sum(scaled * own_columns(hat, targets[shift], 1), axis=-1),
            ],
            axis=1,
        )
    means = sums
    for shift in range(1, parts):
        means = means + exchange(sums, shift)
    means = means / (width * parts)
    d_normed = totals[0]
    for term in received:
        d_normed = d_normed + term.astype(jnp.float32)
    d_hat = d_normed * own_columns(input_norm_gain, me, 0)
    result = inverse * (d_hat - means[:, :1] - own_columns(hat, me, 1) * means[:, 1:])
    return result.astype(jnp.bfloat16)


def solution(mesh):
    return jax.shard_map(
        body,
        mesh=mesh,
        in_specs=(
            P("dp", "tensor"),
            P("dp", "tensor"),
            P(),
            P(),
            P(),
            P(None, "dp", "tensor"),
            P("tensor", "dp"),
            P("tensor", None, None),
        ),
        out_specs=P("dp", "tensor"),
        check_vma=False,
    )
```

```python
import functools
import math

import jax
import jax.numpy as jnp
from jax import lax
from jax.experimental import pallas as pl
from jax.experimental.pallas import tpu as pltpu
from jax.sharding import PartitionSpec as P

HD = 128
SEQ = 256
BLK = 64
EPS = 1e-06


def attention_kernel(heads, ksel, pattern_ref, q_gain_ref, k_gain_ref, qkv_ref, up_ref, out_ref):
    width = heads * HD
    scale = 1.0 / math.sqrt(HD)
    q_gain = q_gain_ref[...]
    k_gain = k_gain_ref[...]
    blocks = SEQ // BLK
    column_block = lax.broadcasted_iota(jnp.int32, (BLK, SEQ), 1) // BLK

    def normalize(values):
        centred = values - jnp.mean(values, axis=-1, keepdims=True)
        inverse = lax.rsqrt(jnp.mean(centred * centred, axis=-1, keepdims=True) + EPS)
        return centred * inverse, inverse

    def pull_back(grad, hat, inverse, gain):
        d_hat = grad * gain
        return inverse * (
            d_hat
            - jnp.mean(d_hat, axis=-1, keepdims=True)
            - hat * jnp.mean(d_hat * hat, axis=-1, keepdims=True)
        )

    def dot(a, b, dims, precision=None):
        return lax.dot_general(
            a, b, (dims, ((), ())), precision=precision, preferred_element_type=jnp.float32
        )

    for head in range(heads):
        lo = head * HD
        q_hat, q_inverse = normalize(qkv_ref[:, lo : lo + HD].astype(jnp.float32))
        k_hat, k_inverse = normalize(
            qkv_ref[:, width + lo : width + lo + HD].astype(jnp.float32)
        )
        value = qkv_ref[:, 2 * width + lo : 2 * width + lo + HD]
        upstream = up_ref[:, lo : lo + HD]
        q_normed = q_hat * q_gain
        k_normed = k_hat * k_gain
        scores = dot(q_normed * scale, k_normed, ((1,), (1,)), lax.Precision.HIGHEST)
        rows = []
        for i in range(blocks):
            hit = column_block == pattern_ref[(head * blocks + i) * ksel]
            for s in range(1, ksel):
                hit = hit | (column_block == pattern_ref[(head * blocks + i) * ksel + s])
            rows.append(jnp.where(hit, jnp.exp(scores[i * BLK : (i + 1) * BLK]), 0.0))
        weights = jnp.concatenate(rows, axis=0)
        probs = weights / jnp.sum(weights, axis=-1, keepdims=True)
        d_probs = dot(upstream, value, ((1,), (1,)))
        d_value = dot(probs.astype(jnp.bfloat16), upstream, ((0,), (0,)))
        d_scores = probs * (d_probs - jnp.sum(probs * d_probs, axis=-1, keepdims=True))
        d_scores = (d_scores * scale).astype(jnp.bfloat16)
        d_q = dot(d_scores, k_normed.astype(jnp.bfloat16), ((1,), (0,)))
        d_k = dot(d_scores, q_normed.astype(jnp.bfloat16), ((0,), (0,)))
        out_ref[:, lo : lo + HD] = pull_back(d_q, q_hat, q_inverse, q_gain).astype(jnp.bfloat16)
        out_ref[:, width + lo : width + lo + HD] = pull_back(
            d_k, k_hat, k_inverse, k_gain
        ).astype(jnp.bfloat16)
        out_ref[:, 2 * width + lo : 2 * width + lo + HD] = d_value.astype(jnp.bfloat16)


def attention_grads(qkv, upstream, q_gain, k_gain, pattern):
    rows, width = upstream.shape
    heads = width // HD
    images = rows // SEQ
    return pl.pallas_call(
        functools.partial(attention_kernel, heads, pattern.shape[2]),
        grid=(images,),
        out_shape=jax.ShapeDtypeStruct((rows, 3 * width), jnp.bfloat16),
        in_specs=[
            pl.BlockSpec(memory_space=pltpu.SMEM),
            pl.BlockSpec((1, HD), lambda i: (0, 0)),
            pl.BlockSpec((1, HD), lambda i: (0, 0)),
            pl.BlockSpec((SEQ, 3 * width), lambda i: (i, 0)),
            pl.BlockSpec((SEQ, width), lambda i: (i, 0)),
        ],
        out_specs=pl.BlockSpec((SEQ, 3 * width), lambda i: (i, 0)),
        cost_estimate=pl.CostEstimate(
            flops=images * heads * 20 * SEQ * SEQ * HD,
            bytes_accessed=rows * width * 14,
            transcendentals=images * heads * SEQ * SEQ,
        ),
    )(pattern.reshape(-1), q_gain.reshape(1, HD), k_gain.reshape(1, HD), qkv, upstream)


def piece_kernel(qkv_ref, out_ref, piece_ref):
    width = qkv_ref.shape[2]
    for part in range(3):
        piece_ref[:, part * width : (part + 1) * width] = qkv_ref[part]
    piece_ref[:, 3 * width :] = out_ref[...].T


def weight_piece(w_qkv, w_out, start, size):
    depth = w_qkv.shape[1]
    width = size * HD
    cols = slice(start * HD, start * HD + width)
    return pl.pallas_call(
        piece_kernel,
        out_shape=jax.ShapeDtypeStruct((depth, 4 * width), w_qkv.dtype),
        cost_estimate=pl.CostEstimate(
            flops=0, bytes_accessed=16 * depth * width, transcendentals=0
        ),
    )(w_qkv[:, :, cols], w_out[cols])


def head_chunks(heads):
    sizes = []
    left = heads - 1
    while left > 0:
        take = min(4, left)
        sizes.append(take)
        left -= take
    return sizes + [1]


def body(tokens, grad_out, input_norm_gain, q_gain, k_gain, w_qkv, w_out, pattern):
    row_count, width = tokens.shape
    parts = lax.axis_size("tensor")
    me = lax.axis_index("tensor")
    local_heads = w_qkv.shape[2] // HD

    gathered = []
    start = 0
    sizes = head_chunks(local_heads)
    for size in sizes:
        piece = weight_piece(w_qkv, w_out, start, size)
        w_qkv, w_out, piece = lax.optimization_barrier((w_qkv, w_out, piece))
        gathered.append(lax.all_gather(piece, "dp", axis=0, tiled=True))
        start += size

    def exchange(value, shift):
        return lax.ppermute(
            value, "tensor", [(source, (source + shift) % parts) for source in range(parts)]
        )

    def whole_rows(own):
        full = jnp.zeros((row_count, width * parts), own.dtype)
        full = lax.dynamic_update_slice_in_dim(full, own, me * width, 1)
        for shift in range(1, parts):
            full = lax.dynamic_update_slice_in_dim(
                full, exchange(own, shift), lax.rem(me + parts - shift, parts) * width, 1
            )
        return full

    values = whole_rows(tokens).astype(jnp.float32)
    grads_full = whole_rows(grad_out)
    centre = jnp.mean(values, axis=-1, keepdims=True)
    centred = values - centre
    inverse = lax.rsqrt(jnp.mean(centred * centred, axis=-1, keepdims=True) + EPS)
    hat = centred * inverse
    normed = (hat * input_norm_gain).astype(jnp.bfloat16)
    normed, grads_full = lax.optimization_barrier((normed, grads_full))

    def own_columns(array, index, axis):
        return lax.dynamic_slice_in_dim(array, index * width, width, axis)

    targets = [lax.rem(me + shift, parts) for shift in range(parts)]
    totals = [None] * parts
    start = 0
    for size, weight in zip(sizes, gathered):
        span = size * HD
        qkv = jnp.dot(
            normed, weight[:, : 3 * span], preferred_element_type=jnp.float32
        ).astype(jnp.bfloat16)
        upstream = jnp.dot(
            grads_full, weight[:, 3 * span :], preferred_element_type=jnp.float32
        ).astype(jnp.bfloat16)
        d_qkv = attention_grads(
            qkv, upstream, q_gain, k_gain, pattern[start : start + size]
        )
        for shift in [*range(1, parts), 0]:
            term = lax.dot_general(
                d_qkv,
                own_columns(weight, targets[shift], 0)[:, : 3 * span],
                (((1,), (1,)), ((), ())),
                preferred_element_type=jnp.float32,
            )
            totals[shift] = term if totals[shift] is None else totals[shift] + term
        start += size
        if start < local_heads:
            normed, grads_full, totals = lax.optimization_barrier((normed, grads_full, totals))

    received = [exchange(totals[shift].astype(jnp.bfloat16), shift) for shift in range(1, parts)]
    sums = jnp.zeros((row_count, 2), jnp.float32)
    for shift in range(parts):
        gain = own_columns(input_norm_gain, targets[shift], 0)
        scaled = totals[shift] * gain
        sums = sums + jnp.stack(
            [
                jnp.sum(scaled, axis=-1),
                jnp.sum(scaled * own_columns(hat, targets[shift], 1), axis=-1),
            ],
            axis=1,
        )
    means = sums
    for shift in range(1, parts):
        means = means + exchange(sums, shift)
    means = means / (width * parts)
    d_normed = totals[0]
    for term in received:
        d_normed = d_normed + term.astype(jnp.float32)
    d_hat = d_normed * own_columns(input_norm_gain, me, 0)
    result = inverse * (d_hat - means[:, :1] - own_columns(hat, me, 1) * means[:, 1:])
    return result.astype(jnp.bfloat16)


def solution(mesh):
    return jax.shard_map(
        body,
        mesh=mesh,
        in_specs=(
            P("dp", "tensor"),
            P("dp", "tensor"),
            P(),
            P(),
            P(),
            P(None, "dp", "tensor"),
            P("tensor", "dp"),
            P("tensor", None, None),
        ),
        out_specs=P("dp", "tensor"),
        check_vma=False,
    )
```

```python
import functools
import math

import jax
import jax.numpy as jnp
from jax import lax
from jax.experimental import pallas as pl
from jax.experimental.pallas import tpu as pltpu
from jax.sharding import PartitionSpec as P

HD = 128
SEQ = 256
BLK = 64
EPS = 1e-06


def attention_kernel(ksel, pattern_ref, q_gain_ref, k_gain_ref, qkv_ref, up_ref, out_ref):
    head = pl.program_id(1)
    scale = 1.0 / math.sqrt(HD)
    q_gain = q_gain_ref[...]
    k_gain = k_gain_ref[...]
    blocks = SEQ // BLK
    column_block = lax.broadcasted_iota(jnp.int32, (BLK, SEQ), 1) // BLK

    def normalize(values):
        centred = values - jnp.mean(values, axis=-1, keepdims=True)
        inverse = lax.rsqrt(jnp.mean(centred * centred, axis=-1, keepdims=True) + EPS)
        return centred * inverse, inverse

    def pull_back(grad, hat, inverse, gain):
        d_hat = grad * gain
        return inverse * (
            d_hat
            - jnp.mean(d_hat, axis=-1, keepdims=True)
            - hat * jnp.mean(d_hat * hat, axis=-1, keepdims=True)
        )

    def dot(a, b, dims, precision=None):
        return lax.dot_general(
            a, b, (dims, ((), ())), precision=precision, preferred_element_type=jnp.float32
        )

    q_hat, q_inverse = normalize(qkv_ref[:, :HD].astype(jnp.float32))
    k_hat, k_inverse = normalize(qkv_ref[:, HD : 2 * HD].astype(jnp.float32))
    value = qkv_ref[:, 2 * HD :]
    upstream = up_ref[...]
    q_normed = q_hat * q_gain
    k_normed = k_hat * k_gain
    scores = dot(q_normed * scale, k_normed, ((1,), (1,)), lax.Precision.HIGHEST)
    rows = []
    for i in range(blocks):
        hit = column_block == pattern_ref[(head * blocks + i) * ksel]
        for s in range(1, ksel):
            hit = hit | (column_block == pattern_ref[(head * blocks + i) * ksel + s])
        rows.append(jnp.where(hit, jnp.exp(scores[i * BLK : (i + 1) * BLK]), 0.0))
    weights = jnp.concatenate(rows, axis=0)
    probs = weights / jnp.sum(weights, axis=-1, keepdims=True)
    d_probs = dot(upstream, value, ((1,), (1,)))
    d_value = dot(probs.astype(jnp.bfloat16), upstream, ((0,), (0,)))
    d_scores = probs * (d_probs - jnp.sum(probs * d_probs, axis=-1, keepdims=True))
    d_scores = (d_scores * scale).astype(jnp.bfloat16)
    d_q = dot(d_scores, k_normed.astype(jnp.bfloat16), ((1,), (0,)))
    d_k = dot(d_scores, q_normed.astype(jnp.bfloat16), ((0,), (0,)))
    out_ref[:, :HD] = pull_back(d_q, q_hat, q_inverse, q_gain).astype(jnp.bfloat16)
    out_ref[:, HD : 2 * HD] = pull_back(d_k, k_hat, k_inverse, k_gain).astype(jnp.bfloat16)
    out_ref[:, 2 * HD :] = d_value.astype(jnp.bfloat16)


def attention_grads(qkv, upstream, q_gain, k_gain, pattern):
    rows, width = upstream.shape
    heads = width // HD
    images = rows // SEQ
    return pl.pallas_call(
        functools.partial(attention_kernel, pattern.shape[2]),
        grid=(images, heads),
        out_shape=jax.ShapeDtypeStruct((rows, 3 * width), jnp.bfloat16),
        in_specs=[
            pl.BlockSpec(memory_space=pltpu.SMEM),
            pl.BlockSpec((1, HD), lambda i, h: (0, 0)),
            pl.BlockSpec((1, HD), lambda i, h: (0, 0)),
            pl.BlockSpec((SEQ, 3 * HD), lambda i, h: (i, h)),
            pl.BlockSpec((SEQ, HD), lambda i, h: (i, h)),
        ],
        out_specs=pl.BlockSpec((SEQ, 3 * HD), lambda i, h: (i, h)),
        cost_estimate=pl.CostEstimate(
            flops=images * heads * 20 * SEQ * SEQ * HD,
            bytes_accessed=rows * width * 14,
            transcendentals=images * heads * SEQ * SEQ,
        ),
    )(pattern.reshape(-1), q_gain.reshape(1, HD), k_gain.reshape(1, HD), qkv, upstream)


def piece_kernel(sizes, qkv_ref, out_ref, *piece_refs):
    start = 0
    for size, piece_ref in zip(sizes, piece_refs):
        for head in range(size):
            cols = slice((start + head) * HD, (start + head + 1) * HD)
            for part in range(3):
                lo = (3 * head + part) * HD
                piece_ref[:, lo : lo + HD] = qkv_ref[part, :, cols]
        cols = slice(start * HD, (start + size) * HD)
        piece_ref[:, 3 * size * HD :] = out_ref[cols, :].T
        start += size


def weight_pieces(w_qkv, w_out, sizes):
    depth, width = w_qkv.shape[1:]
    step = HD if depth % HD == 0 else depth
    return pl.pallas_call(
        functools.partial(piece_kernel, sizes),
        grid=(depth // step,),
        out_shape=[
            jax.ShapeDtypeStruct((depth, 4 * size * HD), w_qkv.dtype) for size in sizes
        ],
        in_specs=[
            pl.BlockSpec((3, step, width), lambda i: (0, i, 0)),
            pl.BlockSpec((width, step), lambda i: (0, i)),
        ],
        out_specs=[pl.BlockSpec((step, 4 * size * HD), lambda i: (i, 0)) for size in sizes],
        cost_estimate=pl.CostEstimate(
            flops=0, bytes_accessed=16 * depth * width, transcendentals=0
        ),
    )(w_qkv, w_out)


def head_chunks(heads):
    last = max(1, heads // 4)
    return [size for size in (heads - last, last) if size > 0]


def body(tokens, grad_out, input_norm_gain, q_gain, k_gain, w_qkv, w_out, pattern):
    row_count, width = tokens.shape
    parts = lax.axis_size("tensor")
    me = lax.axis_index("tensor")
    local_heads = w_qkv.shape[2] // HD

    sizes = head_chunks(local_heads)
    pieces = weight_pieces(w_qkv, w_out, sizes)
    gathered = [lax.all_gather(piece, "dp", axis=0, tiled=True) for piece in pieces]

    def exchange(value, shift):
        return lax.ppermute(
            value, "tensor", [(source, (source + shift) % parts) for source in range(parts)]
        )

    def whole_rows(own):
        full = jnp.zeros((row_count, width * parts), own.dtype)
        full = lax.dynamic_update_slice_in_dim(full, own, me * width, 1)
        for shift in range(1, parts):
            full = lax.dynamic_update_slice_in_dim(
                full, exchange(own, shift), lax.rem(me + parts - shift, parts) * width, 1
            )
        return full

    values = whole_rows(tokens).astype(jnp.float32)
    grads_full = whole_rows(grad_out)
    centre = jnp.mean(values, axis=-1, keepdims=True)
    centred = values - centre
    inverse = lax.rsqrt(jnp.mean(centred * centred, axis=-1, keepdims=True) + EPS)
    hat = centred * inverse
    normed = (hat * input_norm_gain).astype(jnp.bfloat16)
    normed, grads_full = lax.optimization_barrier((normed, grads_full))

    def own_columns(array, index, axis):
        return lax.dynamic_slice_in_dim(array, index * width, width, axis)

    targets = [lax.rem(me + shift, parts) for shift in range(parts)]
    totals = [None] * parts
    start = 0
    for size, weight in zip(sizes, gathered):
        span = size * HD
        qkv = jnp.dot(
            normed, weight[:, : 3 * span], preferred_element_type=jnp.float32
        ).astype(jnp.bfloat16)
        upstream = jnp.dot(
            grads_full, weight[:, 3 * span :], preferred_element_type=jnp.float32
        ).astype(jnp.bfloat16)
        d_qkv = attention_grads(
            qkv, upstream, q_gain, k_gain, pattern[start : start + size]
        )
        for shift in [*range(1, parts), 0]:
            term = lax.dot_general(
                d_qkv,
                own_columns(weight, targets[shift], 0)[:, : 3 * span],
                (((1,), (1,)), ((), ())),
                preferred_element_type=jnp.float32,
            )
            totals[shift] = term if totals[shift] is None else totals[shift] + term
        start += size
        if start < local_heads:
            normed, grads_full, totals = lax.optimization_barrier((normed, grads_full, totals))

    received = [exchange(totals[shift].astype(jnp.bfloat16), shift) for shift in range(1, parts)]
    sums = jnp.zeros((row_count, 2), jnp.float32)
    for shift in range(parts):
        gain = own_columns(input_norm_gain, targets[shift], 0)
        scaled = totals[shift] * gain
        sums = sums + jnp.stack(
            [
                jnp.sum(scaled, axis=-1),
                jnp.sum(scaled * own_columns(hat, targets[shift], 1), axis=-1),
            ],
            axis=1,
        )
    means = sums
    for shift in range(1, parts):
        means = means + exchange(sums, shift)
    means = means / (width * parts)
    d_normed = totals[0]
    for term in received:
        d_normed = d_normed + term.astype(jnp.float32)
    d_hat = d_normed * own_columns(input_norm_gain, me, 0)
    result = inverse * (d_hat - means[:, :1] - own_columns(hat, me, 1) * means[:, 1:])
    return result.astype(jnp.bfloat16)


def solution(mesh):
    return jax.shard_map(
        body,
        mesh=mesh,
        in_specs=(
            P("dp", "tensor"),
            P("dp", "tensor"),
            P(),
            P(),
            P(),
            P(None, "dp", "tensor"),
            P("tensor", "dp"),
            P("tensor", None, None),
        ),
        out_specs=P("dp", "tensor"),
        check_vma=False,
    )
```

```python
import functools
import math

import jax
import jax.numpy as jnp
from jax import lax
from jax.experimental import pallas as pl
from jax.experimental.pallas import tpu as pltpu
from jax.sharding import PartitionSpec as P

HD = 128
SEQ = 256
BLK = 64
EPS = 1e-06


def attention_kernel(ksel, pattern_ref, q_gain_ref, k_gain_ref, qkv_ref, up_ref, out_ref):
    head = pl.program_id(1)
    scale = 1.0 / math.sqrt(HD)
    q_gain = q_gain_ref[...]
    k_gain = k_gain_ref[...]
    blocks = SEQ // BLK
    column_block = lax.broadcasted_iota(jnp.int32, (BLK, SEQ), 1) // BLK

    def normalize(values):
        centred = values - jnp.mean(values, axis=-1, keepdims=True)
        inverse = lax.rsqrt(jnp.mean(centred * centred, axis=-1, keepdims=True) + EPS)
        return centred * inverse, inverse

    def pull_back(grad, hat, inverse, gain):
        d_hat = grad * gain
        return inverse * (
            d_hat
            - jnp.mean(d_hat, axis=-1, keepdims=True)
            - hat * jnp.mean(d_hat * hat, axis=-1, keepdims=True)
        )

    def dot(a, b, dims, precision=None):
        return lax.dot_general(
            a, b, (dims, ((), ())), precision=precision, preferred_element_type=jnp.float32
        )

    q_hat, q_inverse = normalize(qkv_ref[:, :HD].astype(jnp.float32))
    k_hat, k_inverse = normalize(qkv_ref[:, HD : 2 * HD].astype(jnp.float32))
    value = qkv_ref[:, 2 * HD :]
    upstream = up_ref[...]
    q_normed = q_hat * q_gain
    k_normed = k_hat * k_gain
    scores = dot(q_normed * scale, k_normed, ((1,), (1,)), lax.Precision.HIGHEST)
    rows = []
    for i in range(blocks):
        hit = column_block == pattern_ref[(head * blocks + i) * ksel]
        for s in range(1, ksel):
            hit = hit | (column_block == pattern_ref[(head * blocks + i) * ksel + s])
        rows.append(jnp.where(hit, jnp.exp(scores[i * BLK : (i + 1) * BLK]), 0.0))
    weights = jnp.concatenate(rows, axis=0)
    probs = weights / jnp.sum(weights, axis=-1, keepdims=True)
    d_probs = dot(upstream, value, ((1,), (1,)))
    d_value = dot(probs.astype(jnp.bfloat16), upstream, ((0,), (0,)))
    d_scores = probs * (d_probs - jnp.sum(probs * d_probs, axis=-1, keepdims=True))
    d_scores = (d_scores * scale).astype(jnp.bfloat16)
    d_q = dot(d_scores, k_normed.astype(jnp.bfloat16), ((1,), (0,)))
    d_k = dot(d_scores, q_normed.astype(jnp.bfloat16), ((0,), (0,)))
    out_ref[:, :HD] = pull_back(d_q, q_hat, q_inverse, q_gain).astype(jnp.bfloat16)
    out_ref[:, HD : 2 * HD] = pull_back(d_k, k_hat, k_inverse, k_gain).astype(jnp.bfloat16)
    out_ref[:, 2 * HD :] = d_value.astype(jnp.bfloat16)


def attention_grads(qkv, upstream, q_gain, k_gain, pattern):
    rows, width = upstream.shape
    heads = width // HD
    images = rows // SEQ
    return pl.pallas_call(
        functools.partial(attention_kernel, pattern.shape[2]),
        grid=(images, heads),
        out_shape=jax.ShapeDtypeStruct((rows, 3 * width), jnp.bfloat16),
        in_specs=[
            pl.BlockSpec(memory_space=pltpu.SMEM),
            pl.BlockSpec((1, HD), lambda i, h: (0, 0)),
            pl.BlockSpec((1, HD), lambda i, h: (0, 0)),
            pl.BlockSpec((SEQ, 3 * HD), lambda i, h: (i, h)),
            pl.BlockSpec((SEQ, HD), lambda i, h: (i, h)),
        ],
        out_specs=pl.BlockSpec((SEQ, 3 * HD), lambda i, h: (i, h)),
        cost_estimate=pl.CostEstimate(
            flops=images * heads * 20 * SEQ * SEQ * HD,
            bytes_accessed=rows * width * 14,
            transcendentals=images * heads * SEQ * SEQ,
        ),
    )(pattern.reshape(-1), q_gain.reshape(1, HD), k_gain.reshape(1, HD), qkv, upstream)


def piece_kernel(sizes, qkv_ref, out_ref, *piece_refs):
    start = 0
    for size, piece_ref in zip(sizes, piece_refs):
        for head in range(size):
            cols = slice((start + head) * HD, (start + head + 1) * HD)
            for part in range(3):
                lo = (3 * head + part) * HD
                piece_ref[:, lo : lo + HD] = qkv_ref[part, :, cols]
        cols = slice(start * HD, (start + size) * HD)
        piece_ref[:, 3 * size * HD :] = out_ref[cols, :].T
        start += size


def weight_pieces(w_qkv, w_out, sizes):
    depth, width = w_qkv.shape[1:]
    step = HD if depth % HD == 0 else depth
    return pl.pallas_call(
        functools.partial(piece_kernel, sizes),
        grid=(depth // step,),
        out_shape=[
            jax.ShapeDtypeStruct((depth, 4 * size * HD), w_qkv.dtype) for size in sizes
        ],
        in_specs=[
            pl.BlockSpec((3, step, width), lambda i: (0, i, 0)),
            pl.BlockSpec((width, step), lambda i: (0, i)),
        ],
        out_specs=[pl.BlockSpec((step, 4 * size * HD), lambda i: (i, 0)) for size in sizes],
        cost_estimate=pl.CostEstimate(
            flops=0, bytes_accessed=16 * depth * width, transcendentals=0
        ),
    )(w_qkv, w_out)


def projection_kernel(steps, rows_ref, grads_ref, weight_ref, qkv_ref, up_ref, qkv_sum, up_sum):
    step = pl.program_id(0)
    span = qkv_ref.shape[1]

    @pl.when(step == 0)
    def _():
        qkv_sum[...] = jnp.zeros_like(qkv_sum)
        up_sum[...] = jnp.zeros_like(up_sum)

    qkv_sum[...] += jnp.dot(
        rows_ref[...], weight_ref[:, :span], preferred_element_type=jnp.float32
    )
    up_sum[...] += jnp.dot(
        grads_ref[...], weight_ref[:, span:], preferred_element_type=jnp.float32
    )

    @pl.when(step == steps - 1)
    def _():
        qkv_ref[...] = qkv_sum[...].astype(qkv_ref.dtype)
        up_ref[...] = up_sum[...].astype(up_ref.dtype)


def project(normed, grads, weight):
    rows, depth = normed.shape
    width = weight.shape[1] // 4
    block = 1024 if depth % 1024 == 0 else depth
    steps = depth // block
    return pl.pallas_call(
        functools.partial(projection_kernel, steps),
        grid=(steps,),
        out_shape=[
            jax.ShapeDtypeStruct((rows, 3 * width), jnp.bfloat16),
            jax.ShapeDtypeStruct((rows, width), jnp.bfloat16),
        ],
        in_specs=[
            pl.BlockSpec((rows, block), lambda k: (0, k)),
            pl.BlockSpec((rows, block), lambda k: (0, k)),
            pl.BlockSpec((block, 4 * width), lambda k: (k, 0)),
        ],
        out_specs=[
            pl.BlockSpec((rows, 3 * width), lambda k: (0, 0)),
            pl.BlockSpec((rows, width), lambda k: (0, 0)),
        ],
        scratch_shapes=[
            pltpu.VMEM((rows, 3 * width), jnp.float32),
            pltpu.VMEM((rows, width), jnp.float32),
        ],
        compiler_params=pltpu.CompilerParams(vmem_limit_bytes=32 * 1024 * 1024),
        cost_estimate=pl.CostEstimate(
            flops=8 * rows * depth * width,
            bytes_accessed=8 * depth * width + 4 * rows * depth,
            transcendentals=0,
        ),
    )(normed, grads, weight)


def head_chunks(heads):
    last = max(1, heads // 4)
    return [size for size in (heads - last, last) if size > 0]


def body(tokens, grad_out, input_norm_gain, q_gain, k_gain, w_qkv, w_out, pattern):
    row_count, width = tokens.shape
    parts = lax.axis_size("tensor")
    me = lax.axis_index("tensor")
    local_heads = w_qkv.shape[2] // HD

    sizes = head_chunks(local_heads)
    pieces = weight_pieces(w_qkv, w_out, sizes)
    gathered = [lax.all_gather(piece, "dp", axis=0, tiled=True) for piece in pieces]

    def exchange(value, shift):
        return lax.ppermute(
            value, "tensor", [(source, (source + shift) % parts) for source in range(parts)]
        )

    def whole_rows(own):
        full = jnp.zeros((row_count, width * parts), own.dtype)
        full = lax.dynamic_update_slice_in_dim(full, own, me * width, 1)
        for shift in range(1, parts):
            full = lax.dynamic_update_slice_in_dim(
                full, exchange(own, shift), lax.rem(me + parts - shift, parts) * width, 1
            )
        return full

    values = whole_rows(tokens).astype(jnp.float32)
    grads_full = whole_rows(grad_out)
    centre = jnp.mean(values, axis=-1, keepdims=True)
    centred = values - centre
    inverse = lax.rsqrt(jnp.mean(centred * centred, axis=-1, keepdims=True) + EPS)
    hat = centred * inverse
    normed = (hat * input_norm_gain).astype(jnp.bfloat16)
    normed, grads_full = lax.optimization_barrier((normed, grads_full))

    def own_columns(array, index, axis):
        return lax.dynamic_slice_in_dim(array, index * width, width, axis)

    targets = [lax.rem(me + shift, parts) for shift in range(parts)]
    totals = [None] * parts
    received = []
    start = 0
    for size, weight in zip(sizes, gathered):
        span = size * HD
        last = start + size == local_heads
        if last:
            qkv, upstream = project(normed, grads_full, weight)
        else:
            qkv = jnp.dot(
                normed, weight[:, : 3 * span], preferred_element_type=jnp.float32
            ).astype(jnp.bfloat16)
            upstream = jnp.dot(
                grads_full, weight[:, 3 * span :], preferred_element_type=jnp.float32
            ).astype(jnp.bfloat16)
        d_qkv = attention_grads(
            qkv, upstream, q_gain, k_gain, pattern[start : start + size]
        )
        for shift in [*range(1, parts), 0]:
            term = lax.dot_general(
                d_qkv,
                own_columns(weight, targets[shift], 0)[:, : 3 * span],
                (((1,), (1,)), ((), ())),
                preferred_element_type=jnp.float32,
            )
            totals[shift] = term if totals[shift] is None else totals[shift] + term
            if last and shift:
                outgoing, totals[shift], d_qkv = lax.optimization_barrier(
                    (totals[shift].astype(jnp.bfloat16), totals[shift], d_qkv)
                )
                received.append(exchange(outgoing, shift))
        start += size
        if not last:
            normed, grads_full, totals = lax.optimization_barrier((normed, grads_full, totals))

    sums = jnp.zeros((row_count, 2), jnp.float32)
    for shift in range(parts):
        gain = own_columns(input_norm_gain, targets[shift], 0)
        scaled = totals[shift] * gain
        sums = sums + jnp.stack(
            [
                jnp.sum(scaled, axis=-1),
                jnp.sum(scaled * own_columns(hat, targets[shift], 1), axis=-1),
            ],
            axis=1,
        )
    means = sums
    for shift in range(1, parts):
        means = means + exchange(sums, shift)
    means = means / (width * parts)
    d_normed = totals[0]
    for term in received:
        d_normed = d_normed + term.astype(jnp.float32)
    d_hat = d_normed * own_columns(input_norm_gain, me, 0)
    result = inverse * (d_hat - means[:, :1] - own_columns(hat, me, 1) * means[:, 1:])
    return result.astype(jnp.bfloat16)


def solution(mesh):
    return jax.shard_map(
        body,
        mesh=mesh,
        in_specs=(
            P("dp", "tensor"),
            P("dp", "tensor"),
            P(),
            P(),
            P(),
            P(None, "dp", "tensor"),
            P("tensor", "dp"),
            P("tensor", None, None),
        ),
        out_specs=P("dp", "tensor"),
        check_vma=False,
    )
```
